32 devices in a mesh: dp: 16 (over z, x, core), mp: 2 (over y).
Axes of the slice: x: 2, y: 2, z: 4, core: 2. Of those that a mesh axis runs over, the one named last changes fastest.
Arguments:
- lang: bfloat16 [15360, 768], P(('dp', 'mp')), may hold values from -6 to 6
- vision: bfloat16 [27648, 768], P(('dp', 'mp')), may hold values from -6 to 6
- region_count: int32 [768], P('dp'), may hold values from 10 to 36, as said below
- att_in: bfloat16 [3, 3, 768, 768], P(None, None, None, 'mp'), may hold values from -0.3125 to 0.3125
- att_in_bias: bfloat16 [3, 2, 768], P(None, None, 'mp'), may hold values from -3 to 3
- att_out: bfloat16 [3, 768, 768], P(None, 'mp'), may hold values from -0.5 to 0.5
- att_row_bias: bfloat16 [3, 2, 768], replicated, may hold values from -3 to 3
- att_gain: bfloat16 [3, 768], replicated, may hold values from 0.25 to 1.75
- ffn_up: bfloat16 [2, 768, 3072], P(None, None, 'mp'), may hold values from -0.21875 to 0.21875
- ffn_up_bias: bfloat16 [2, 3072], P(None, 'mp'), may hold values from -3 to 3
- ffn_down: bfloat16 [2, 3072, 768], P(None, 'mp'), may hold values from -0.15625 to 0.15625
- ffn_row_bias: bfloat16 [2, 2, 768], replicated, may hold values from -3 to 3
- ffn_gain: bfloat16 [2, 768], replicated, may hold values from 0.25 to 1.75
- cot_lang: bfloat16 [15360, 768], P(('dp', 'mp')), may hold values from -6 to 6
- cot_vision: bfloat16 [27648, 768], P(('dp', 'mp')), may hold values from -6 to 6
Outputs:
- out_lang: float32 [15360, 768], P(('dp', 'mp'))
- out_vision: float32 [27648, 768], P(('dp', 'mp'))
- grad_lang: float32 [15360, 768], P(('dp', 'mp'))
- grad_vision: float32 [27648, 768], P(('dp', 'mp'))
- grad_att_in: float32 [3, 3, 768, 768], P(None, None, 'dp', 'mp')
- grad_att_in_bias: float32 [3, 2, 768], replicated
- grad_att_out: float32 [3, 768, 768], P(None, 'mp', 'dp')
- grad_att_row_bias: float32 [3, 2, 768], replicated
- grad_att_gain: float32 [3, 768], replicated
- grad_ffn_up: float32 [2, 768, 3072], P(None, 'dp', 'mp')
- grad_ffn_up_bias: float32 [2, 3072], replicated
- grad_ffn_down: float32 [2, 3072, 768], P(None, 'mp', 'dp')
- grad_ffn_row_bias: float32 [2, 2, 768], replicated
- grad_ffn_gain: float32 [2, 768], replicated
The draws below stay inside these ranges and needn't reach their ends.
Inputs may be any that keep to these rules, and one draw needn't show every extreme that they name: `region_count`: real regions of each item; its slots from that count up to 36 are padding. Some item has 36 and some has 10.
All inputs are finite; a program needn't handle non-finite values.
Results may differ from the reference program's by a relative error of at most 0.029.
The reference program's roundings to bfloat16 on the way count: a program that leaves them out, or rounds other values in their place, can miss the bound.
Values may be sent and summed in bfloat16 or wider, within the bound.
No kernel may reach another device: no remote copies, remote signals or barrier semaphores. Data moves between devices by JAX's collectives and lax.ppermute only.
A program may use at most 320 MiB of HBM per device.

```python
from functools import partial
import jax
import jax.numpy as jnp
from jax import lax

D = 768
HEADS = 12
FF = 3072
WORDS = 20
REGIONS = 36
ITEM_DEV = 48
HEAD_DIM = 64
ITEMS = 768
N_DP = 16


def draw_region_count(key, part):
    first, second, third, fourth, fifth = jax.random.split(key, 5)
    draw_one = jax.random.randint(first, (ITEMS,), 0, REGIONS - 9)
    draw_two = jax.random.randint(second, (ITEMS,), 0, REGIONS - 9)
    draw_three = jax.random.randint(third, (ITEMS,), 0, REGIONS - 9)
    counts = 10 + jnp.minimum(jnp.minimum(draw_one, draw_two), draw_three)
    highest = jax.random.randint(fourth, (), 0, ITEMS)
    lowest = (highest + 1 + jax.random.randint(fifth, (), 0, ITEMS - 1)) % ITEMS
    places = jnp.arange(ITEMS, dtype=jnp.int32)
    counts = jnp.where(places == highest, REGIONS, counts)
    counts = jnp.where(places == lowest, 10, counts)
    return counts.astype(jnp.int32)


def strengthened(result, key, source, target, blocks, factor):
    owner, partner = [(jnp.arange(result.shape[dim]) // (result.shape[dim] // blocks)).reshape([-1 if axis == dim else 1 for axis in range(result.ndim)]) for dim in (source, target)]
    chosen = jax.random.permutation(key, blocks)[partner]
    strong = (owner == chosen) | (owner == (partner + blocks // 2) % blocks)
    return jnp.where(strong, factor * result, result)


def levels(own_key, extent, cuts, least, top_value):
    loudness = 1.0
    for dim, parts in cuts:
        draws = jax.random.uniform(jax.random.fold_in(jax.random.fold_in(own_key, 6), dim), (parts,), jnp.float32, least / len(cuts), top_value / len(cuts))
        loudness = loudness * jnp.repeat(jnp.exp(draws), extent[dim] // parts).reshape((-1,) + (1,) * (len(extent) - 1 - dim))
    return loudness


def gaussian(own_key, dims, scale, bound, cuts=(), held_as=jnp.bfloat16):
    drawn = scale * jax.random.normal(own_key, dims, jnp.float32)
    if cuts:
        drawn = drawn * levels(own_key, dims, cuts, -0.22, 0.18)
    return jnp.clip(drawn, -bound, bound).astype(held_as)


def noise_with(own_key, dims, scale, bound, cuts, heavy, held_as=jnp.bfloat16):
    entries = scale * jax.random.normal(own_key, dims, jnp.float32)
    if cuts:
        entries = entries * levels(own_key, dims, cuts, -0.22, 0.18)
    return jnp.clip(strengthened(entries, jax.random.fold_in(own_key, 3), *heavy), -bound, bound).astype(held_as)


def setup_inputs(seed: int = 0) -> dict:
    splits = jax.random.split(jax.random.key(seed), 16)
    return {
        "lang": noise_with(splits[0], (ITEMS * WORDS, D), 1.0, 6.0, ((0, 32),), (0, 1, 32, 2.75)),
        "vision": noise_with(splits[1], (ITEMS * REGIONS, D), 1.0, 6.0, ((0, 32),), (0, 1, 32, 2.75)),
        "region_count": draw_region_count(jax.random.fold_in(splits[15], 71), 0),
        "att_in": gaussian(splits[3], (3, 3, D, D), (D // 2) ** -0.5, 0.3125, ((3, 2),)),
        "att_in_bias": gaussian(splits[4], (3, 2, D), 0.5, 3.0, ((2, 2),)),
        "att_out": gaussian(splits[5], (3, D, D), (D // 6) ** -0.5, 0.5, ((1, 2),)),
        "att_row_bias": gaussian(splits[6], (3, 2, D), 0.5, 3.0),
        "att_gain": jnp.clip(1.0 + 0.15 * jax.random.normal(splits[7], (3, D), jnp.float32), 0.25, 1.75).astype(jnp.bfloat16),
        "ffn_up": gaussian(splits[8], (2, D, FF), D ** -0.5, 0.21875, ((2, 2),)),
        "ffn_up_bias": gaussian(splits[9], (2, FF), 0.5, 3.0, ((1, 2),)),
        "ffn_down": gaussian(splits[10], (2, FF, D), (FF // 2) ** -0.5, 0.15625, ((1, 2),)),
        "ffn_row_bias": gaussian(splits[11], (2, 2, D), 0.5, 3.0),
        "ffn_gain": jnp.clip(1.0 + 0.15 * jax.random.normal(splits[12], (2, D), jnp.float32), 0.25, 1.75).astype(jnp.bfloat16),
        "cot_lang": noise_with(splits[13], (ITEMS * WORDS, D), 1.0, 6.0, ((0, 32),), (0, 1, 32, 2.75)),
        "cot_vision": noise_with(splits[14], (ITEMS * REGIONS, D), 1.0, 6.0, ((0, 32),), (0, 1, 32, 2.75)),
    }


NORM_EPSILON = 1e-06
MASK_FILL = -1000000000.0

@jax.custom_vjp
def low(v):
    return lax.optimization_barrier(v.astype(jnp.bfloat16)).astype(jnp.float32)

@jax.custom_vjp
def low_back(v):
    return v

def low_keep(v):
    return (low(v), None)

def low_pass(kept, grad):
    return (grad,)

def back_keep(v):
    return (v, None)

def back_low(kept, grad):
    return (low(grad),)
low.defvjp(low_keep, low_pass)
low_back.defvjp(back_keep, back_low)

def matmul(left, right):
    return jnp.dot(left, right, precision=lax.Precision.HIGHEST)

def normalize(summed, gain, shift):
    row_mean = lax.optimization_barrier(jnp.mean(summed, axis=-1, keepdims=True))
    centred = summed - row_mean
    spread = lax.optimization_barrier(jnp.mean(centred * centred, axis=-1, keepdims=True))
    return centred * lax.rsqrt(spread + NORM_EPSILON) * gain + shift

def split_heads(matrix):
    return matrix.reshape(matrix.shape[0], matrix.shape[1], HEADS, HEAD_DIM)

def attend(query_rows, context_rows, key_ok, weight_in, bias_in, weight_out):
    queries = low_back(low(matmul(query_rows, weight_in[0]) + bias_in[0]))
    key_rows = low_back(low(matmul(context_rows, weight_in[1])))
    values = low_back(low(matmul(context_rows, weight_in[2]) + bias_in[1]))
    scores = jnp.einsum('nahd,nchd->nhac', split_heads(queries), split_heads(key_rows), precision=lax.Precision.HIGHEST)
    scores = low_back(scores * HEAD_DIM ** (-0.5))
    scores = jnp.where(key_ok[:, None, None, :], scores, MASK_FILL)
    probability = low(jax.nn.softmax(scores, axis=-1))
    mixed_rows = jnp.einsum('nhac,nchd->nahd', probability, split_heads(values), precision=lax.Precision.HIGHEST)
    mixed_rows = low_back(low(mixed_rows.reshape(queries.shape)))
    return low_back(matmul(mixed_rows, weight_out))

def layer(region_ok, lang, vision, att_in, att_in_bias, att_out, att_row_bias, att_gain, ffn_up, ffn_up_bias, ffn_down, ffn_row_bias, ffn_gain):
    word_ok = jnp.ones(lang.shape[:2], dtype=bool)

    def attention(block_index, stream, query_rows, context_rows, key_ok):
        branch = attend(query_rows, context_rows, key_ok, att_in[block_index], att_in_bias[block_index], att_out[block_index])
        return normalize(stream + branch + att_row_bias[block_index, 0], att_gain[block_index], att_row_bias[block_index, 1])

    def feed(block_index, stream):
        row_data = low(stream)
        hidden = low_back(matmul(row_data, ffn_up[block_index]) + ffn_up_bias[block_index])
        activated = low(jax.nn.gelu(hidden, approximate=False))
        branch = low_back(matmul(activated, ffn_down[block_index]))
        return normalize(stream + branch + ffn_row_bias[block_index, 0], ffn_gain[block_index], ffn_row_bias[block_index, 1])
    lang_low = low(lang)
    vision_low = low(vision)
    lang_one = attention(0, lang, lang_low, vision_low, region_ok)
    vision_one = attention(0, vision, vision_low, lang_low, word_ok)
    lang_low = low(lang_one)
    lang_two = attention(1, lang_one, lang_low, lang_low, word_ok)
    vision_low = low(vision_one)
    vision_two = attention(2, vision_one, vision_low, vision_low, region_ok)
    return (feed(0, lang_two), feed(1, vision_two))

def reference(lang, vision, region_count, att_in, att_in_bias, att_out, att_row_bias, att_gain, ffn_up, ffn_up_bias, ffn_down, ffn_row_bias, ffn_gain, cot_lang, cot_vision):
    params = tuple((array_in.astype(jnp.float32) for array_in in (att_in, att_in_bias, att_out, att_row_bias, att_gain, ffn_up, ffn_up_bias, ffn_down, ffn_row_bias, ffn_gain)))
    groups = (lang.astype(jnp.float32).reshape(N_DP, ITEM_DEV, WORDS, D), vision.astype(jnp.float32).reshape(N_DP, ITEM_DEV, REGIONS, D), region_count.reshape(N_DP, ITEM_DEV), cot_lang.astype(jnp.float32).reshape(N_DP, ITEM_DEV, WORDS, D), cot_vision.astype(jnp.float32).reshape(N_DP, ITEM_DEV, REGIONS, D))
    slot_index = jnp.arange(REGIONS, dtype=jnp.int32)

    def one_group(running, group):
        lang_group, vision_group, count_group, cot_words, cot_regions = group
        region_ok = slot_index[None, :] < count_group[:, None]
        cot_regions = cot_regions * region_ok[:, :, None].astype(jnp.float32)
        outputs, pull_back = jax.vjp(partial(layer, region_ok), lang_group, vision_group, *params)
        gradients = pull_back((cot_words, cot_regions))
        running = tuple((earlier + gradient for earlier, gradient in zip(running, gradients[2:])))
        return (running, (outputs[0], outputs[1], gradients[0], gradients[1]))
    start = tuple((jnp.zeros_like(weight) for weight in params))
    totals, (out_words, out_regions, grad_words, grad_regions) = lax.scan(one_group, start, groups)
    return (out_words.reshape(ITEMS * WORDS, D), out_regions.reshape(ITEMS * REGIONS, D), grad_words.reshape(ITEMS * WORDS, D), grad_regions.reshape(ITEMS * REGIONS, D), totals[0], totals[1], totals[2], totals[3], totals[4], totals[5], totals[6], totals[7], totals[8], totals[9])
```

```python
from functools import partial

import jax
import jax.numpy as jnp
from jax import lax
from jax.experimental import pallas as pl
from jax.experimental.pallas import tpu as pltpu
from jax.sharding import PartitionSpec as P

D = 768
FF = 3072
WORDS = 20
REGIONS = 36
HEAD_DIM = 64
GROUP = 4
PIECES = 4

NORM_EPSILON = 1e-06
MASK_FILL = -1000000000.0
F32 = jnp.float32
BF16 = jnp.bfloat16


def dot32(left, right, left_dim, right_dim):
    return lax.dot_general(
        left, right, (((left_dim,), (right_dim,)), ((), ())), preferred_element_type=F32
    )


def item_rows(rows, per_item):
    row = lax.broadcasted_iota(jnp.int32, (rows, 1), 0)
    item = jnp.zeros((rows, 1), jnp.int32)
    for bound in range(per_item, rows, per_item):
        item = item + (row >= bound).astype(jnp.int32)
    return item


def two_heads(block):
    lane = lax.broadcasted_iota(jnp.int32, block.shape, 1)
    zero = jnp.zeros_like(block)
    return jnp.concatenate(
        (jnp.where(lane < HEAD_DIM, block, zero), jnp.where(lane < HEAD_DIM, zero, block)), axis=0
    )


def join_heads(stacked):
    rows = stacked.shape[0] // 2
    lane = lax.broadcasted_iota(jnp.int32, (rows, stacked.shape[1]), 1)
    return jnp.where(lane < HEAD_DIM, stacked[:rows], stacked[rows:])


def probabilities(query_stack, keys, ok_stack):
    scores = dot32(query_stack, keys, 1, 1) * HEAD_DIM ** (-0.5)
    scores = jnp.where(ok_stack, scores, MASK_FILL)
    raised = jnp.exp(scores - jnp.max(scores, axis=-1, keepdims=True))
    return raised * (1.0 / jnp.sum(raised, axis=-1, keepdims=True))


def attend_pairs_forward(q_ref, k_ref, v_ref, ok, o_ref):
    ok_stack = jnp.concatenate((ok, ok), axis=0)
    for start in range(0, q_ref.shape[1], 2 * HEAD_DIM):
        span = slice(start, start + 2 * HEAD_DIM)
        probs = probabilities(two_heads(q_ref[:, span]), k_ref[:, span], ok_stack)
        mixed = dot32(probs.astype(BF16), v_ref[:, span], 1, 0)
        o_ref[:, span] = join_heads(mixed).astype(BF16)


def attend_pairs_backward(q_ref, k_ref, v_ref, d_ref, ok, dq_ref, dk_ref, dv_ref):
    ok_stack = jnp.concatenate((ok, ok), axis=0)
    scale = HEAD_DIM ** (-0.5)
    for start in range(0, q_ref.shape[1], 2 * HEAD_DIM):
        span = slice(start, start + 2 * HEAD_DIM)
        query_stack = two_heads(q_ref[:, span])
        keys = k_ref[:, span]
        probs = probabilities(query_stack, keys, ok_stack)
        grad_stack = two_heads(d_ref[:, span])
        grad_probs = dot32(grad_stack, v_ref[:, span], 1, 1)
        centre = jnp.sum(grad_probs * probs, axis=-1, keepdims=True)
        grad_scores = (probs * (grad_probs - centre)).astype(BF16)
        dq_ref[:, span] = (join_heads(dot32(grad_scores, keys, 1, 0)) * scale).astype(BF16)
        dk_ref[:, span] = (dot32(grad_scores, query_stack, 0, 0) * scale).astype(BF16)
        dv_ref[:, span] = dot32(probs.astype(BF16), grad_stack, 0, 0).astype(BF16)


def group_masks(region_key, cross, words, regions):
    lang_item = item_rows(words, WORDS)
    vision_item = item_rows(regions, REGIONS)
    lane = lax.broadcasted_iota(jnp.int32, (1, words), 1)
    word_key = jnp.zeros((1, words), jnp.int32)
    for bound in range(WORDS, words, WORDS):
        word_key = word_key + (lane >= bound).astype(jnp.int32)
    if cross:
        return lang_item == region_key, vision_item == word_key
    return lang_item == word_key, vision_item == region_key


def attention_forward_kernel(cross, key_ref, ql, kl, vl, qv, kv, vv, ol, ov):
    lang_ok, vision_ok = group_masks(key_ref[0], cross, ql.shape[0], qv.shape[0])
    if cross:
        attend_pairs_forward(ql, kv, vv, lang_ok, ol)
        attend_pairs_forward(qv, kl, vl, vision_ok, ov)
    else:
        attend_pairs_forward(ql, kl, vl, lang_ok, ol)
        attend_pairs_forward(qv, kv, vv, vision_ok, ov)


def attention_backward_kernel(
    cross, key_ref, ql, kl, vl, qv, kv, vv, dol, dov, dql, dkl, dvl, dqv, dkv, dvv
):
    lang_ok, vision_ok = group_masks(key_ref[0], cross, ql.shape[0], qv.shape[0])
    if cross:
        attend_pairs_backward(ql, kv, vv, dol, lang_ok, dql, dkv, dvv)
        attend_pairs_backward(qv, kl, vl, dov, vision_ok, dqv, dkl, dvl)
    else:
        attend_pairs_backward(ql, kl, vl, dol, lang_ok, dql, dkl, dvl)
        attend_pairs_backward(qv, kv, vv, dov, vision_ok, dqv, dkv, dvv)


def attention_call(kernel, cross, region_key, arrays, out_streams):
    groups = region_key.shape[0]
    width = arrays[0].shape[1]
    rows = {"l": GROUP * WORDS, "v": GROUP * REGIONS}

    def spec(stream):
        return pl.BlockSpec((rows[stream], width), lambda g: (g, 0))

    streams = "lllvvv" + ("lv" if len(arrays) == 8 else "")
    flops = 24 * 64 * 2 * 8 * groups * GROUP * 100
    return pl.pallas_call(
        partial(kernel, cross),
        grid=(groups,),
        in_specs=[pl.BlockSpec((1, 1, rows["v"]), lambda g: (g, 0, 0))]
        + [spec(stream) for stream in streams],
        out_specs=[spec(stream) for stream in out_streams],
        out_shape=[
            jax.ShapeDtypeStruct((groups * rows[stream], width), BF16) for stream in out_streams
        ],
        cost_estimate=pl.CostEstimate(
            flops=flops * 100, bytes_accessed=30_000_000, transcendentals=1_000_000
        ),
    )(region_key, *arrays)


def norm_forward(summed, gain, shift):
    row_mean = jnp.mean(summed, axis=-1, keepdims=True)
    centred = summed - row_mean
    spread = jnp.mean(centred * centred, axis=-1, keepdims=True)
    inv_scale = lax.rsqrt(spread + NORM_EPSILON)
    normed = centred * inv_scale
    return (normed * gain.astype(F32) + shift, (normed, inv_scale))


def norm_backward(grad_out, saved, gain):
    normed, inv_scale = saved
    grad_normed = grad_out * gain.astype(F32)
    mean_first = jnp.mean(grad_normed, axis=-1, keepdims=True)
    mean_second = jnp.mean(grad_normed * normed, axis=-1, keepdims=True)
    grad_total = inv_scale * (grad_normed - mean_first - normed * mean_second)
    return (grad_total, jnp.sum(grad_out * normed, axis=0), jnp.sum(grad_out, axis=0))


class Links:
    def __init__(self):
        self.ndp = lax.axis_size("dp")
        self.dp = lax.axis_index("dp")
        self.mp = lax.axis_index("mp")
        self.piece = self.dp % PIECES

    def across(self, value):
        pairs = [(2 * d + m, 2 * d + 1 - m) for d in range(self.ndp) for m in range(2)]
        return lax.ppermute(value, ("dp", "mp"), pairs)

    def flip(self, value, bit):
        pairs = [
            (2 * d + m, 2 * (d ^ (1 << bit)) + m) for d in range(self.ndp) for m in range(2)
        ]
        return lax.ppermute(value, ("dp", "mp"), pairs)

    def other_pieces(self, own_piece):
        first = self.across(own_piece)
        third = self.flip(first, 1)
        second = self.flip(first, 0)
        fourth = self.flip(third, 0)
        return [first, second, third, fourth]

    def place(self, pieces, axis):
        size = pieces[0].shape[axis]
        shape = list(pieces[0].shape)
        shape[axis] = size * PIECES
        whole = jnp.zeros(shape, pieces[0].dtype)
        for step, part in enumerate(pieces):
            whole = lax.dynamic_update_slice_in_dim(
                whole, part, (self.piece ^ step) * size, axis
            )
        return whole

    def own_pieces(self, value, axis):
        size = value.shape[axis] // PIECES
        return [
            lax.dynamic_slice_in_dim(value, (self.piece ^ step) * size, size, axis)
            for step in range(PIECES)
        ]

    def own_piece(self, value, axis):
        size = value.shape[axis] // PIECES
        return lax.dynamic_slice_in_dim(value, self.piece * size, size, axis)

    def reduce(self, own, other, moved):
        rows, columns = own.shape
        low = rows // self.ndp
        side = self.dp % 2

        def halves(value, side, count):
            split = value.reshape(count // 2, 2, low, value.shape[-1])
            keep = lax.dynamic_index_in_dim(split, side, 1, keepdims=False)
            send = lax.dynamic_index_in_dim(split, 1 - side, 1, keepdims=False)
            return keep, send.astype(BF16)

        def swapped(value, bit):
            if not moved or bit > 1:
                return value
            split = value.reshape(*value.shape[:-1], 2, 2, columns // 4)
            flipped = split[..., ::-1, :] if bit == 0 else split[..., ::-1, :, :]
            return flipped.reshape(value.shape)

        keep_own, send_own = halves(own, side, self.ndp)
        keep_other, send_other = halves(other, side, self.ndp)
        got_other = self.flip(send_other, 0)
        got_own = self.flip(send_own, 0)
        other_sum = keep_other + swapped(got_other, 0).astype(F32)
        total = keep_own + swapped(got_own, 0).astype(F32)
        total = total + self.across(other_sum.astype(BF16)).astype(F32)
        bit, count = 1, self.ndp // 2
        while count > 1:
            side = (self.dp >> bit) % 2
            keep, send = halves(total, side, count)
            total = keep + swapped(self.flip(send, bit), bit).astype(F32)
            bit, count = bit + 1, count // 2
        return total.reshape(low, columns)

    def settle(self, value):
        size = value.shape[-1] // PIECES
        return jnp.concatenate(
            [
                lax.dynamic_slice_in_dim(value, (self.piece ^ step) * size, size, -1)
                for step in range(PIECES)
            ],
            axis=-1,
        )

    def total(self, value):
        value = value + self.across(value)
        for bit in range(self.ndp.bit_length() - 1):
            value = value + self.flip(value, bit)
        return value


def project(rows, weight, bias):
    queries = (dot32(rows, weight[0], 1, 0) + bias[0].astype(F32)).astype(BF16)
    keys = dot32(rows, weight[1], 1, 0).astype(BF16)
    values = (dot32(rows, weight[2], 1, 0) + bias[1].astype(F32)).astype(BF16)
    return queries, keys, values


def attention_block(low_pair, halves_pair, cross, region_key):
    kept, branch_lang, branch_vision = [], 0.0, 0.0
    for lang_half, vision_half in zip(*halves_pair):
        lang_proj = project(low_pair[0], lang_half[0], lang_half[2])
        vision_proj = project(low_pair[1], vision_half[0], vision_half[2])
        mixed = attention_call(
            attention_forward_kernel, cross, region_key, (*lang_proj, *vision_proj), "lv"
        )
        branch_lang = branch_lang + dot32(mixed[0], lang_half[1], 1, 0)
        branch_vision = branch_vision + dot32(mixed[1], vision_half[1], 1, 0)
        kept.append((lang_proj, vision_proj, mixed))
    return (branch_lang, branch_vision), kept


def attention_block_backward(grad_pair, low_pair, halves_pair, kept, cross, region_key):
    grads = tuple(g.astype(BF16) for g in grad_pair)
    back_lang, back_vision = 0.0, 0.0
    per_half = []
    for (lang_half, vision_half), (lang_proj, vision_proj, mixed) in zip(
        zip(*halves_pair), kept
    ):
        out_grads = [dot32(g, m, 0, 0) for g, m in zip(grads, mixed)]
        dmix = [
            dot32(g, half[1], 1, 1).astype(BF16)
            for g, half in zip(grads, (lang_half, vision_half))
        ]
        back = attention_call(
            attention_backward_kernel,
            cross,
            region_key,
            (*lang_proj, *vision_proj, *dmix),
            "lllvvv",
        )
        lang_d, vision_d = back[:3], back[3:]
        in_grads = [
            [dot32(low, d, 0, 0) for d in ds] for low, ds in zip(low_pair, (lang_d, vision_d))
        ]
        bias_grads = [
            jnp.stack([jnp.sum(ds[k].astype(F32), axis=0) for k in (0, 2)])
            for ds in (lang_d, vision_d)
        ]
        for k in range(3):
            back_lang = back_lang + dot32(lang_d[k], lang_half[0][k], 1, 1)
            back_vision = back_vision + dot32(vision_d[k], vision_half[0][k], 1, 1)
        per_half.append((in_grads, out_grads, bias_grads))
    return (back_lang, back_vision), per_half


def gelu_back(hidden, act_grad):
    pull_back = jax.vjp(partial(jax.nn.gelu, approximate=False), hidden)[1]
    return pull_back(act_grad)[0].astype(BF16)


def per_device(
    lang,
    vision,
    region_count,
    att_in,
    att_in_bias,
    att_out,
    att_row_bias,
    att_gain,
    ffn_up,
    ffn_up_bias,
    ffn_down,
    ffn_row_bias,
    ffn_gain,
    cot_lang,
    cot_vision,
):
    links = Links()
    items = region_count.shape[0] // 2
    groups = items // GROUP
    counts = lax.dynamic_slice_in_dim(region_count, links.mp * items, items)
    slot = jnp.arange(REGIONS, dtype=jnp.int32)
    region_ok = slot[None, :] < counts[:, None]
    item_index = (jnp.arange(items, dtype=jnp.int32) % GROUP)[:, None]
    region_key = jnp.where(region_ok, item_index, -1).reshape(groups, 1, GROUP * REGIONS)
    row_ok = region_ok.reshape(-1, 1).astype(F32)

    heads = att_in.shape[-1]
    units = ffn_up.shape[-1]
    small_own = jnp.concatenate((att_in_bias.reshape(-1), ffn_up_bias.reshape(-1)))
    small_other = links.across(small_own)
    bias_other = small_other[: 6 * heads].reshape(3, 2, heads)
    up_bias_other = small_other[6 * heads :].reshape(2, units)
    att_halves = []
    for block in range(3):
        in_other = links.place(links.other_pieces(links.own_piece(att_in[block], 1)), 1)
        out_other = links.place(links.other_pieces(links.own_piece(att_out[block], 0)), 0)
        att_halves.append(
            (
                (att_in[block], att_out[block], att_in_bias[block]),
                (in_other, out_other, bias_other[block]),
            )
        )
    up_own = links.own_pieces(ffn_up, 2)
    down_own = links.own_pieces(ffn_down, 1)
    up_other = links.other_pieces(up_own[0])
    down_other = links.other_pieces(down_own[0])
    ups = [jnp.concatenate(part, axis=2) for part in (up_own, up_other)]
    downs = [jnp.concatenate(part, axis=1) for part in (down_own, down_other)]
    up_biases = [
        jnp.concatenate(links.own_pieces(bias, 1), axis=1)
        for bias in (ffn_up_bias, up_bias_other)
    ]

    row_bias = att_row_bias.astype(F32)
    ffn_bias = ffn_row_bias.astype(F32)
    cross_halves = (att_halves[0], att_halves[0])
    self_halves = (att_halves[1], att_halves[2])

    branches, cross_kept = attention_block((lang, vision), cross_halves, True, region_key)
    lang_one, lang_norm_a = norm_forward(
        lang.astype(F32) + branches[0] + row_bias[0, 0], att_gain[0], row_bias[0, 1]
    )
    vision_one, vision_norm_a = norm_forward(
        vision.astype(F32) + branches[1] + row_bias[0, 0], att_gain[0], row_bias[0, 1]
    )
    low_one = (lang_one.astype(BF16), vision_one.astype(BF16))
    branches, self_kept = attention_block(low_one, self_halves, False, region_key)
    lang_two, lang_norm_b = norm_forward(
        lang_one + branches[0] + row_bias[1, 0], att_gain[1], row_bias[1, 1]
    )
    vision_two, vision_norm_b = norm_forward(
        vision_one + branches[1] + row_bias[2, 0], att_gain[2], row_bias[2, 1]
    )
    low_two = (lang_two.astype(BF16), vision_two.astype(BF16))

    outs, ffn_grads, streams = [], [], []
    cots = (cot_lang.astype(F32), cot_vision.astype(F32) * row_ok)
    for stream, (low, full, cot) in enumerate(zip(low_two, (lang_two, vision_two), cots)):
        hidden = [
            dot32(low, up[stream], 1, 0) + bias[stream].astype(F32)
            for up, bias in zip(ups, up_biases)
        ]
        act = [jax.nn.gelu(h, approximate=False).astype(BF16) for h in hidden]
        branch = sum(dot32(a, down[stream], 1, 0) for a, down in zip(act, downs))
        out, saved = norm_forward(
            full + branch + ffn_bias[stream, 0], ffn_gain[stream], ffn_bias[stream, 1]
        )
        outs.append(out)
        total, gain_grad, shift_grad = norm_backward(cot, saved, ffn_gain[stream])
        low_grad = total.astype(BF16)
        back = total
        down_grads, up_grads, up_bias_grads = [], [], []
        for part in range(2):
            dhidden = gelu_back(hidden[part], dot32(low_grad, downs[part][stream], 1, 1))
            down_grads.append(dot32(low_grad, act[part], 0, 0))
            up_grads.append(dot32(low, dhidden, 0, 0))
            up_bias_grads.append(jnp.sum(dhidden.astype(F32), axis=0))
            back = back + dot32(dhidden, ups[part][stream], 1, 1)
        ffn_grads.append(
            (
                links.reduce(down_grads[0], down_grads[1], True),
                links.reduce(up_grads[0], up_grads[1], True),
                up_bias_grads,
                jnp.stack((jnp.sum(total, axis=0), shift_grad)),
                gain_grad,
            )
        )
        streams.append(back)

    lang_total, lang_gain_b, lang_shift_b = norm_backward(streams[0], lang_norm_b, att_gain[1])
    vision_total, vision_gain_b, vision_shift_b = norm_backward(
        streams[1], vision_norm_b, att_gain[2]
    )
    lang_rows_b = jnp.stack((jnp.sum(lang_total, axis=0), lang_shift_b))
    vision_rows_b = jnp.stack((jnp.sum(vision_total, axis=0), vision_shift_b))
    back, self_grads = attention_block_backward(
        (lang_total, vision_total), low_one, self_halves, self_kept, False, region_key
    )
    in_reduced, out_reduced, bias_parts = [None] * 3, [None] * 3, [None] * 3
    for stream in range(2):
        own, other = self_grads
        own_in = jnp.concatenate(own[0][stream], axis=1)
        other_in = jnp.concatenate(other[0][stream], axis=1)
        in_reduced[1 + stream] = links.reduce(own_in, other_in, False)
        out_reduced[1 + stream] = links.reduce(own[1][stream], other[1][stream], False)
        bias_parts[1 + stream] = (own[2][stream], other[2][stream])
    lang_back = lang_total + back[0]
    vision_back = vision_total + back[1]
    lang_total, lang_gain_a, lang_shift_a = norm_backward(lang_back, lang_norm_a, att_gain[0])
    vision_total, vision_gain_a, vision_shift_a = norm_backward(
        vision_back, vision_norm_a, att_gain[0]
    )
    cross_rows = jnp.stack(
        (jnp.sum(lang_total, axis=0) + jnp.sum(vision_total, axis=0), lang_shift_a + vision_shift_a)
    )
    back, cross_grads = attention_block_backward(
        (lang_total, vision_total), (lang, vision), cross_halves, cross_kept, True, region_key
    )
    grad_lang = lang_total + back[0]
    grad_vision = vision_total + back[1]
    own, other = cross_grads
    in_reduced[0] = links.reduce(
        jnp.concatenate([a + b for a, b in zip(*own[0])], axis=1),
        jnp.concatenate([a + b for a, b in zip(*other[0])], axis=1),
        False,
    )
    out_reduced[0] = links.reduce(own[1][0] + own[1][1], other[1][0] + other[1][1], False)
    bias_parts[0] = (own[2][0] + own[2][1], other[2][0] + other[2][1])

    low_rows = D // links.ndp
    att_in_grad = jnp.stack(
        [part.reshape(low_rows, 3, heads).transpose(1, 0, 2) for part in in_reduced]
    )
    att_out_grad = jnp.stack([part.T for part in out_reduced])
    down_grad = jnp.stack([links.settle(part[0]).T for part in ffn_grads])
    up_grad = jnp.stack([links.settle(part[1]) for part in ffn_grads])

    def whole(own, other, width):
        lead = own.shape[:-1]
        result = jnp.zeros((*lead, 2 * width), F32)
        zeros = (0,) * len(lead)
        result = lax.dynamic_update_slice(result, own, (*zeros, links.mp * width))
        return lax.dynamic_update_slice(result, other, (*zeros, (1 - links.mp) * width))

    in_bias = whole(
        jnp.stack([part[0] for part in bias_parts]),
        jnp.stack([part[1] for part in bias_parts]),
        heads,
    )
    up_bias = whole(
        *(links.settle(jnp.stack([part[2][h] for part in ffn_grads])) for h in range(2)), units
    )
    parts = (
        in_bias,
        up_bias,
        jnp.stack((cross_rows, lang_rows_b, vision_rows_b)),
        jnp.stack((lang_gain_a + vision_gain_a, lang_gain_b, vision_gain_b)),
        jnp.stack([part[3] for part in ffn_grads]),
        jnp.stack([part[4] for part in ffn_grads]),
    )
    flat = links.total(jnp.concatenate([part.reshape(-1) for part in parts]))
    summed, at = [], 0
    for part in parts:
        summed.append(flat[at : at + part.size].reshape(part.shape))
        at += part.size
    return (
        outs[0],
        outs[1],
        grad_lang,
        grad_vision,
        att_in_grad,
        summed[0],
        att_out_grad,
        summed[2],
        summed[3],
        up_grad,
        summed[1],
        down_grad,
        summed[4],
        summed[5],
    )


def solution(mesh):
    rows = P(("dp", "mp"), None)
    return jax.shard_map(
        per_device,
        mesh=mesh,
        in_specs=(
            rows,
            rows,
            P("dp"),
            P(None, None, None, "mp"),
            P(None, None, "mp"),
            P(None, "mp", None),
            P(),
            P(),
            P(None, None, "mp"),
            P(None, "mp"),
            P(None, "mp", None),
            P(),
            P(),
            rows,
            rows,
        ),
        out_specs=(
            rows,
            rows,
            rows,
            rows,
            P(None, None, "dp", "mp"),
            P(),
            P(None, "mp", "dp"),
            P(),
            P(),
            P(None, "dp", "mp"),
            P(),
            P(None, "mp", "dp"),
            P(),
            P(),
        ),
        check_vma=False,
    )
```

```python
from functools import partial
import math

import jax
import jax.numpy as jnp
from jax import lax
from jax.experimental import pallas as pl
from jax.experimental.pallas import tpu as pltpu
from jax.sharding import PartitionSpec as P

D = 768
FF = 3072
HALF = 384
UNITS = 1536
WORDS = 20
REGIONS = 36
HEAD_DIM = 64
GROUP = 4
STEP = 8
PIECES = 4

NORM_EPSILON = 1e-06
MASK_FILL = -1e30
LOG2_E = 1.4426950408889634
SCALE = HEAD_DIM ** (-0.5)
F32 = jnp.float32
BF16 = jnp.bfloat16


def dot32(left, right, left_dim, right_dim):
    return lax.dot_general(
        left, right, (((left_dim,), (right_dim,)), ((), ())), preferred_element_type=F32
    )


def group_index(shape, axis, per_item):
    place = lax.broadcasted_iota(jnp.int32, shape, axis)
    span = per_item * GROUP
    item = jnp.zeros(shape, jnp.int32)
    for bound in range(per_item, shape[axis], per_item):
        if bound % span == 0:
            item = jnp.where(place >= bound, 0, item)
        else:
            item = item + (place >= bound).astype(jnp.int32)
    return item


def two_heads(block):
    lane = lax.broadcasted_iota(jnp.int32, block.shape, 1)
    zero = jnp.zeros_like(block)
    return jnp.concatenate(
        (jnp.where(lane < HEAD_DIM, block, zero), jnp.where(lane < HEAD_DIM, zero, block)), axis=0
    )


def join_heads(stacked):
    rows = stacked.shape[0] // 2
    lane = lax.broadcasted_iota(jnp.int32, (rows, stacked.shape[1]), 1)
    return jnp.where(lane < HEAD_DIM, stacked[:rows], stacked[rows:])


def key_mask(key_item, query_rows, query_item_rows):
    query_item = group_index((1, 2 * query_rows), 1, query_item_rows)
    return jnp.where(key_item == query_item, 0.0, MASK_FILL).astype(F32)


def probabilities(query_stack, keys, mask):
    scores = dot32(keys, query_stack, 1, 1) * (SCALE * LOG2_E) + mask
    raised = jnp.exp2(scores - jnp.max(scores, axis=0, keepdims=True))
    return raised * (1.0 / jnp.sum(raised, axis=0, keepdims=True))


def head_pairs(half):
    return [half * 3 * HALF + start for start in range(0, HALF, 2 * HEAD_DIM)]


def attend_forward(q_ref, kv_ref, o_ref, q_at, k_at, q_rows, k_rows, mask, halves):
    for half in halves:
        for pair, column in enumerate(head_pairs(half)):
            query_stack = two_heads(q_ref[pl.ds(q_at, q_rows), column : column + 128])
            keys = kv_ref[pl.ds(k_at, k_rows), column + HALF : column + HALF + 128]
            values = kv_ref[pl.ds(k_at, k_rows), column + 2 * HALF : column + 2 * HALF + 128]
            probs = probabilities(query_stack, keys, mask).astype(BF16)
            mixed = dot32(probs, values, 0, 0)
            target = half * HALF + pair * 128
            o_ref[pl.ds(q_at, q_rows), target : target + 128] = join_heads(mixed).astype(BF16)


def attend_backward(
    q_ref, kv_ref, do_ref, dq_ref, dkv_ref, q_at, k_at, q_rows, k_rows, mask, halves
):
    for half in halves:
        for pair, column in enumerate(head_pairs(half)):
            query_stack = two_heads(q_ref[pl.ds(q_at, q_rows), column : column + 128])
            keys = kv_ref[pl.ds(k_at, k_rows), column + HALF : column + HALF + 128]
            values = kv_ref[pl.ds(k_at, k_rows), column + 2 * HALF : column + 2 * HALF + 128]
            target = half * HALF + pair * 128
            grad_stack = two_heads(do_ref[pl.ds(q_at, q_rows), target : target + 128])
            probs = probabilities(query_stack, keys, mask)
            grad_probs = dot32(values, grad_stack, 1, 1)
            centre = jnp.sum(grad_probs * probs, axis=0, keepdims=True)
            grad_scores = (probs * (grad_probs - centre)).astype(BF16)
            dq = join_heads(dot32(grad_scores, keys, 0, 0)) * SCALE
            dk = dot32(grad_scores, query_stack, 1, 0) * SCALE
            dv = dot32(probs.astype(BF16), grad_stack, 1, 0)
            dq_ref[pl.ds(q_at, q_rows), column : column + 128] = dq.astype(BF16)
            dkv_ref[pl.ds(k_at, k_rows), column + HALF : column + HALF + 128] = dk.astype(BF16)
            dkv_ref[pl.ds(k_at, k_rows), column + 2 * HALF : column + 2 * HALF + 128] = dv.astype(
                BF16
            )


def attend_streams(cross, key_ref, body):
    rows = (GROUP * WORDS, GROUP * REGIONS)
    per_item = (WORDS, REGIONS)

    def group(index, carry):
        at = [pl.multiple_of(index * count, 16) for count in rows]
        items = (
            group_index((rows[0], 1), 0, WORDS),
            key_ref[pl.ds(at[1], rows[1]), :],
        )
        for query in range(2):
            key = 1 - query if cross else query
            mask = key_mask(items[key], rows[query], per_item[query])
            body(query, key, at[query], at[key], rows[query], rows[key], mask)
        return carry

    lax.fori_loop(0, STEP // GROUP, group, 0)


def norm_forward(summed, gain, shift):
    centred = summed - jnp.mean(summed, axis=-1, keepdims=True)
    spread = jnp.mean(centred * centred, axis=-1, keepdims=True)
    inv_scale = lax.rsqrt(spread + NORM_EPSILON)
    normed = centred * inv_scale
    return normed * gain + shift, normed, inv_scale


def norm_backward(grad_out, normed, inv_scale, gain):
    grad_normed = grad_out * gain
    mean_first = jnp.mean(grad_normed, axis=-1, keepdims=True)
    mean_second = jnp.mean(grad_normed * normed, axis=-1, keepdims=True)
    total = inv_scale * (grad_normed - mean_first - normed * mean_second)
    sums = [jnp.sum(part, axis=0, keepdims=True) for part in (total, grad_out, grad_out * normed)]
    return total, sums


def add_rows(ref, first, rows):
    for row, value in enumerate(rows):
        ref[first + row : first + row + 1, :] += value


def clear_first(*refs):
    @pl.when(pl.program_id(0) == 0)
    def _():
        for ref in refs:
            ref[...] = jnp.zeros(ref.shape, ref.dtype)


def place_other(piece, parts, base, w_in, w_out, in_at, out_at):
    size_in, size_out = D // PIECES, HALF // PIECES
    for step, part in enumerate(parts):
        at = piece ^ step
        rows_in = pl.ds(pl.multiple_of(at * size_in, 16), size_in)
        rows_out = pl.ds(pl.multiple_of(out_at + at * size_out, 16), size_out)
        for kind in range(3):
            column = in_at + kind * HALF
            first = base + kind * size_in
            w_in[rows_in, column : column + HALF] = part[first : first + size_in, :]
        for side in range(2):
            first = base + 3 * size_in + side * size_out
            w_out[rows_out, side * HALF : (side + 1) * HALF] = part[first : first + size_out, :]


def place_own(own_in, own_out, w_in, w_out):
    for kind in range(3):
        w_in[:, kind * HALF : (kind + 1) * HALF] = own_in[0, kind]
    if own_out is not None:
        w_out[0:HALF, :] = own_out[0]


def first_half_kernel(scal, key_ref, xl, xv, own_in, bias, qkvl, qkvv, ol, ov, w_in):
    @pl.when(pl.program_id(0) == 0)
    def _():
        place_own(own_in, None, w_in, None)

    for x, qkv in ((xl, qkvl), (xv, qkvv)):
        qkv[...] = (dot32(x[...], w_in[...], 1, 0) + bias[:, : 3 * HALF]).astype(BF16)
    qkvs, outs = (qkvl, qkvv), (ol, ov)

    def body(query, key, *rest):
        attend_forward(qkvs[query], qkvs[key], outs[query], *rest, (0,))

    attend_streams(True, key_ref, body)


def block_forward_kernel(cross, *refs):
    refs = list(refs)
    take = lambda count: [refs.pop(0) for _ in range(count)]
    sets = 1 if cross else 2
    scal, key_ref = take(2)
    xs = take(2)
    first = take(4) if cross else None
    own = [take(2) for _ in range(sets)]
    parts = take(PIECES)
    biases = take(sets)
    vecs = take(2)
    qkvs, os, ns, invs, lows = (take(2) for _ in range(5))
    weights = [take(2) for _ in range(sets)]

    @pl.when(pl.program_id(0) == 0)
    def _():
        for index in range(sets):
            place_own(*own[index], *weights[index])
            place_other(scal[0], parts, index * D, *weights[index], 3 * HALF, HALF)

    fulls = []
    for stream in range(2):
        w_in = weights[stream % sets][0]
        bias = biases[stream % sets]
        if cross:
            fulls.append(xs[stream][...].astype(F32))
            low = xs[stream][...]
            qkvs[stream][:, : 3 * HALF] = first[2 * stream][...]
            os[stream][:, :HALF] = first[2 * stream + 1][...]
            qkvs[stream][:, 3 * HALF :] = (
                dot32(low, w_in[:, 3 * HALF :], 1, 0) + bias[:, 3 * HALF :]
            ).astype(BF16)
        else:
            vec = vecs[stream]
            low = (xs[stream][...] * vec[3:4, :] + vec[4:5, :]).astype(BF16)
            qkvs[stream][...] = (dot32(low, w_in[...], 1, 0) + bias[...]).astype(BF16)

    def body(query, key, *rest):
        attend_forward(qkvs[query], qkvs[key], os[query], *rest, (1,) if cross else (0, 1))

    attend_streams(cross, key_ref, body)
    for stream in range(2):
        vec = vecs[stream]
        branch = dot32(os[stream][...], weights[stream % sets][1][...], 1, 0)
        full = fulls[stream] if cross else xs[stream][...] * vec[3:4, :] + vec[4:5, :]
        out, normed, inv_scale = norm_forward(full + branch + vec[0:1, :], vec[2:3, :], vec[1:2, :])
        ns[stream][...] = normed
        invs[stream][...] = inv_scale
        lows[stream][...] = out.astype(BF16)


def block_backward_kernel(cross, *refs):
    refs = list(refs)
    take = lambda count: [refs.pop(0) for _ in range(count)]
    sets = 1 if cross else 2
    scal, key_ref = take(2)
    totals, lows, qkvs = take(2), take(2), take(2)
    own = [take(2) for _ in range(sets)]
    parts = take(PIECES)
    if not cross:
        ns, invs, vecs = take(2), take(2), take(2)
    dqkvs, biases, outs = take(2), take(2), take(2)
    if not cross:
        low_outs, sums = take(2), take(1)
    mixes = take(2)
    weights = [take(2) for _ in range(sets)]

    @pl.when(pl.program_id(0) == 0)
    def _():
        for index in range(sets):
            place_own(*own[index], *weights[index])
            place_other(scal[0], parts, index * D, *weights[index], 3 * HALF, HALF)

    clear_first(*biases, *(() if cross else sums))
    for stream in range(2):
        mixes[stream][...] = dot32(
            lows[stream][...], weights[stream % sets][1][...], 1, 1
        ).astype(BF16)

    def body(query, key, *rest):
        attend_backward(
            qkvs[query], qkvs[key], mixes[query], dqkvs[query], dqkvs[key], *rest, (0, 1)
        )

    attend_streams(cross, key_ref, body)
    for stream in range(2):
        grads = dqkvs[stream][...]
        biases[stream][...] += jnp.sum(grads.astype(F32), axis=0, keepdims=True)
        back = totals[stream][...] + dot32(grads, weights[stream % sets][0][...], 1, 1)
        if cross:
            outs[stream][...] = back
        else:
            total, rows = norm_backward(
                back, ns[stream][...], invs[stream][...], vecs[stream][2:3, :]
            )
            outs[stream][...] = total
            low_outs[stream][...] = total.astype(BF16)
            add_rows(sums[0], 0, rows)


CHUNK = 512


def gelu_parts(hidden):
    below = 0.5 + 0.5 * lax.erf(hidden * (0.5**0.5))
    density = jnp.exp2(hidden * hidden * (-0.5 * LOG2_E)) * (1.0 / math.sqrt(2.0 * math.pi))
    return hidden * below, below + hidden * density


def feed_kernel(
    scal,
    n_ref,
    inv_ref,
    low_ref,
    cot_ref,
    ok_ref,
    own_up,
    own_down,
    part0,
    part1,
    part2,
    part3,
    bias,
    vec,
    out_ref,
    act_ref,
    dhid_ref,
    dbr_ref,
    total_ref,
    low_total_ref,
    sums,
    up_sums,
    other_up,
    other_down,
    slope,
):
    @pl.when(pl.program_id(0) == 0)
    def _():
        size = UNITS // PIECES
        for step, part in enumerate((part0, part1, part2, part3)):
            at = pl.multiple_of((scal[0] ^ step) * size, 128)
            other_up[:, pl.ds(at, size)] = part[0:D, :]
            other_down[pl.ds(at, size), 0:HALF] = part[D : D + size, :]
            other_down[pl.ds(at, size), HALF:D] = part[D + size : D + 2 * size, :]

    clear_first(sums, up_sums)

    def up(start):
        if start < UNITS:
            return own_up[0, :, start : start + CHUNK]
        return other_up[:, start - UNITS : start - UNITS + CHUNK]

    def down(start):
        if start < UNITS:
            return own_down[0, start : start + CHUNK, :]
        return other_down[start - UNITS : start - UNITS + CHUNK, :]

    normed = n_ref[...]
    full = normed * vec[0:1, :] + vec[1:2, :]
    low = low_ref[...]
    branch = 0.0
    for start in range(0, FF, CHUNK):
        span = slice(start, start + CHUNK)
        act, slope_part = gelu_parts(dot32(low, up(start), 1, 0) + bias[:, span])
        act = act.astype(BF16)
        act_ref[:, span] = act
        slope[:, span] = slope_part
        branch = branch + dot32(act, down(start), 1, 0)
    out, out_normed, out_scale = norm_forward(full + branch + vec[2:3, :], vec[4:5, :], vec[3:4, :])
    out_ref[...] = out
    cot = cot_ref[...].astype(F32) * ok_ref[...]
    total, rows = norm_backward(cot, out_normed, out_scale, vec[4:5, :])
    add_rows(sums, 0, rows)
    low_grad = total.astype(BF16)
    dbr_ref[...] = low_grad
    back = total
    for start in range(0, FF, CHUNK):
        span = slice(start, start + CHUNK)
        dhidden = (dot32(low_grad, down(start), 1, 1) * slope[:, span]).astype(BF16)
        dhid_ref[:, span] = dhidden
        up_sums[:, span] += jnp.sum(dhidden.astype(F32), axis=0, keepdims=True)
        back = back + dot32(dhidden, up(start), 1, 1)
    total, rows = norm_backward(back, normed, inv_ref[...], vec[0:1, :])
    add_rows(sums, 3, rows)
    total_ref[...] = total
    low_total_ref[...] = total.astype(BF16)


def grads_kernel(plan, counts, scal, *refs):
    operands, (send, keep, total) = refs[:-3], refs[-3:]
    low_rows = send.shape[2]
    at = 0
    for terms, width in plan:
        value = 0.0
        for left, right in terms:
            value = value + dot32(operands[left][...], operands[right][...], 0, 0)
        total[:, 0:width] = value
        for slot in range(send.shape[1]):
            pair = (scal[1] >> 1) ^ slot
            side = scal[1] & 1
            for ref, which in ((keep, side), (send, 1 - side)):
                first = pl.multiple_of((2 * pair + which) * low_rows, 16)
                ref[0, slot, :, at : at + width] = total[pl.ds(first, low_rows), 0:width].astype(
                    BF16
                )
        at += width


def grads_unit(scal, ndp, plan, operands):
    columns = sum(width for _, width in plan)
    low_rows = D // ndp
    if low_rows % 16 or ndp % 2:
        dp = lax.axis_index("dp")
        order = jnp.arange(ndp, dtype=jnp.int32) ^ dp
        halves = []
        for half in range(2):
            parts = []
            for terms, width in plan:
                parts.append(
                    sum(
                        dot32(
                            operands[a], operands[b][:, half * width : (half + 1) * width], 0, 0
                        ).astype(F32)
                        for a, b in terms
                    )
                )
            whole = jnp.concatenate(parts, axis=1).astype(BF16)
            halves.append(whole.reshape(ndp, low_rows, columns)[order])
        slots = jnp.stack(halves).reshape(2, ndp // 2, 2, low_rows, columns)
        return slots[:, :, 1], slots[:, :, 0]
    width_of = {}
    for terms, width in plan:
        for left, right in terms:
            width_of[right] = width
    specs, flops = [], 0
    for index, operand in enumerate(operands):
        if index in width_of:
            specs.append(pl.BlockSpec((operand.shape[0], width_of[index]), lambda m, s: (0, m)))
            flops += 2 * operand.shape[0] * operand.shape[1] * D
        else:
            specs.append(pl.BlockSpec(operand.shape, lambda m, s: (0, 0)))
    shape = (2, ndp // 2, low_rows, columns)
    out = jax.ShapeDtypeStruct(shape, BF16)
    out_spec = pl.BlockSpec((1, *shape[1:]), lambda m, s: (m, 0, 0, 0))
    return pl.pallas_call(
        partial(grads_kernel, plan, None),
        grid_spec=pltpu.PrefetchScalarGridSpec(
            num_scalar_prefetch=1,
            grid=(2,),
            in_specs=specs,
            out_specs=[out_spec, out_spec],
            scratch_shapes=[pltpu.VMEM((D, max(width for _, width in plan)), F32)],
        ),
        out_shape=[out, out],
        cost_estimate=pl.CostEstimate(
            flops=flops, bytes_accessed=20_000_000, transcendentals=0
        ),
        name="grads",
    )(scal, *operands)


def row_spec(rows, width):
    return pl.BlockSpec((rows, width), lambda i, s: (i, 0))


def full_spec(shape, lead=None):
    if lead is None:
        return pl.BlockSpec(shape, lambda i, s: (0,) * len(shape))
    return pl.BlockSpec((1, *shape[1:]), lambda i, s: (lead,) + (0,) * (len(shape) - 1))


def call(kernel, scal, steps, operands, outs, scratch, flops, name):
    nbytes = sum(a.size * a.dtype.itemsize for a, _ in operands)
    return pl.pallas_call(
        kernel,
        grid_spec=pltpu.PrefetchScalarGridSpec(
            num_scalar_prefetch=1,
            grid=(steps,),
            in_specs=[spec for _, spec in operands],
            out_specs=[spec for *_, spec in outs],
            scratch_shapes=scratch,
        ),
        out_shape=[jax.ShapeDtypeStruct(shape, dtype) for shape, dtype, _ in outs],
        cost_estimate=pl.CostEstimate(
            flops=int(flops), bytes_accessed=2 * nbytes, transcendentals=0
        ),
        name=name,
    )(scal, *[array for array, _ in operands])


class Links:
    def __init__(self):
        self.ndp = lax.axis_size("dp")
        self.bits = self.ndp.bit_length() - 1
        self.dp = lax.axis_index("dp")
        self.mp = lax.axis_index("mp")
        self.piece = self.dp % PIECES

    def across(self, value):
        pairs = [(2 * d + m, 2 * d + 1 - m) for d in range(self.ndp) for m in range(2)]
        return lax.ppermute(value, ("dp", "mp"), pairs)

    def flip(self, value, bit):
        pairs = [
            (2 * d + m, 2 * (d ^ (1 << bit)) + m) for d in range(self.ndp) for m in range(2)
        ]
        return lax.ppermute(value, ("dp", "mp"), pairs)

    def exchange(self, value, axis):
        return self.across(value) if axis == "m" else self.flip(value, axis)

    def other_pieces(self, own_piece):
        first = self.across(own_piece)
        third = self.flip(first, 1)
        second = self.flip(first, 0)
        fourth = self.flip(third, 0)
        return [first, second, third, fourth]

    def own_piece(self, value, axis):
        size = value.shape[axis] // PIECES
        return lax.dynamic_slice_in_dim(value, self.piece * size, size, axis)

    def reduce(self, send, keep, order):
        low, columns = send.shape[2:]
        axes = ["m"] + list(range(self.bits - 1, 0, -1))
        shape = (2,) * len(axes) + (low, columns)
        got = self.flip(send, 0).reshape(shape)
        total = keep.reshape(shape).astype(F32) + got.astype(F32)
        for axis in order:
            place = axes.index(axis)
            axes.pop(place)
            going = lax.index_in_dim(total, 1, place, keepdims=False).astype(BF16)
            staying = lax.index_in_dim(total, 0, place, keepdims=False)
            total = staying + self.exchange(going, axis).astype(F32)
        return total

    def total(self, value):
        value = value + self.across(value)
        for bit in range(self.bits):
            value = value + self.flip(value, bit)
        return value


def per_device(
    lang,
    vision,
    region_count,
    att_in,
    att_in_bias,
    att_out,
    att_row_bias,
    att_gain,
    ffn_up,
    ffn_up_bias,
    ffn_down,
    ffn_row_bias,
    ffn_gain,
    cot_lang,
    cot_vision,
):
    links = Links()
    items = region_count.shape[0] // 2
    steps = items // STEP
    rows = (STEP * WORDS, STEP * REGIONS)
    all_rows = (items * WORDS, items * REGIONS)
    row_total = sum(all_rows)
    scal = jnp.stack((links.piece, links.dp)).astype(jnp.int32)
    counts = lax.dynamic_slice_in_dim(region_count, links.mp * items, items)
    slot = jnp.arange(REGIONS, dtype=jnp.int32)
    region_ok = slot[None, :] < counts[:, None]
    item_index = (jnp.arange(items, dtype=jnp.int32) % GROUP)[:, None]
    region_key = jnp.where(region_ok, item_index, -1).reshape(-1, 1)
    row_ok = (region_ok.reshape(-1, 1).astype(F32), jnp.ones((all_rows[0], 1), F32))
    row_ok = (row_ok[1], row_ok[0])

    def att_piece(block):
        piece_in = links.own_piece(att_in[block], 1).reshape(-1, HALF)
        piece_out = links.own_piece(att_out[block], 0)
        return [piece_in, piece_out[:, :HALF], piece_out[:, HALF:]]

    def ffn_piece(stream):
        piece_up = links.own_piece(ffn_up[stream], 1)
        piece_down = links.own_piece(ffn_down[stream], 0)
        return [piece_up, piece_down[:, :HALF], piece_down[:, HALF:]]

    small_own = jnp.concatenate((att_in_bias.reshape(-1), ffn_up_bias.reshape(-1)))
    cross_parts = links.other_pieces(jnp.concatenate(att_piece(0)))
    small_other = links.across(small_own)
    self_parts = links.other_pieces(jnp.concatenate(att_piece(1) + att_piece(2)))
    ffn_parts = [None, None]
    for stream in (1, 0):
        ffn_parts[stream] = links.other_pieces(jnp.concatenate(ffn_piece(stream)))
    bias_other = small_other[: 6 * HALF].reshape(3, 2, HALF)
    up_bias_other = small_other[6 * HALF :].reshape(2, UNITS)

    def bias_row(block):
        none = jnp.zeros((HALF,), BF16)
        own, other = att_in_bias[block], bias_other[block]
        return jnp.concatenate((own[0], none, own[1], other[0], none, other[1]))[None].astype(F32)

    own_row = jnp.concatenate((att_in_bias[0, 0], jnp.zeros((HALF,), BF16), att_in_bias[0, 1]))
    own_row = own_row[None].astype(F32)
    row_bias = att_row_bias.astype(F32)
    gain = att_gain.astype(F32)
    ffn_bias = ffn_row_bias.astype(F32)
    feed_gain = ffn_gain.astype(F32)
    none = jnp.zeros((D,), F32)

    def vectors(*rows8):
        return jnp.stack(list(rows8) + [none] * (8 - len(rows8)))

    key_operand = (region_key, row_spec(rows[1], 1))

    def own_weights(block):
        return [(att_in, full_spec(att_in.shape, block)), (att_out, full_spec(att_out.shape, block))]

    def streams(arrays):
        return [(a, row_spec(rows[s], a.shape[1])) for s, a in enumerate(arrays)]

    def stream_outs(width, dtype):
        return [((all_rows[s], width), dtype, row_spec(rows[s], width)) for s in range(2)]

    def whole(arrays):
        return [(a, full_spec(a.shape)) for a in arrays]

    def weight_scratch(sets):
        return [pltpu.VMEM((D, 6 * HALF), BF16), pltpu.VMEM((D, D), BF16)] * sets

    first = call(
        first_half_kernel,
        scal,
        steps,
        [key_operand] + streams((lang, vision)) + own_weights(0)[:1] + whole([own_row]),
        stream_outs(3 * HALF, BF16) + stream_outs(HALF, BF16),
        [pltpu.VMEM((D, 3 * HALF), BF16)],
        2 * row_total * D * 3 * HALF * 3,
        "cross_first",
    )
    first = (first[0], first[2], first[1], first[3])
    cross_vec = vectors(row_bias[0, 0], row_bias[0, 1], gain[0])
    forward_outs = (
        stream_outs(6 * HALF, BF16)
        + stream_outs(D, BF16)
        + stream_outs(D, F32)
        + stream_outs(1, F32)
        + stream_outs(D, BF16)
    )
    cross_out = call(
        partial(block_forward_kernel, True),
        scal,
        steps,
        [key_operand]
        + streams((lang, vision))
        + [(a, row_spec(rows[i // 2], a.shape[1])) for i, a in enumerate(first)]
        + own_weights(0)
        + whole(cross_parts)
        + whole([bias_row(0), cross_vec, cross_vec]),
        forward_outs,
        weight_scratch(1),
        2 * row_total * D * 5 * HALF * 3,
        "cross_forward",
    )
    qkv_a, o_a, n_a, inv_a, low_a = (cross_out[2 * i : 2 * i + 2] for i in range(5))
    self_vecs = [
        vectors(row_bias[b, 0], row_bias[b, 1], gain[b], gain[0], row_bias[0, 1]) for b in (1, 2)
    ]
    self_out = call(
        partial(block_forward_kernel, False),
        scal,
        steps,
        [key_operand]
        + streams(n_a)
        + own_weights(1)
        + own_weights(2)
        + whole(self_parts)
        + whole([bias_row(1), bias_row(2)] + self_vecs),
        forward_outs,
        weight_scratch(2),
        2 * row_total * D * 8 * HALF * 3,
        "self_forward",
    )
    qkv_b, o_b, n_b, inv_b, low_b = (self_out[2 * i : 2 * i + 2] for i in range(5))

    cots = (cot_lang, cot_vision)
    fed = [None, None]
    reduced_ffn = [None, None]
    for stream in (1, 0):
        bias = jnp.concatenate((ffn_up_bias[stream], up_bias_other[stream]))[None].astype(F32)
        vec = vectors(
            gain[1 + stream],
            row_bias[1 + stream, 1],
            ffn_bias[stream, 0],
            ffn_bias[stream, 1],
            feed_gain[stream],
        )
        tall = rows[stream]

        def spec(width, tall=tall):
            return row_spec(tall, width)

        count = all_rows[stream]
        fed[stream] = call(
            feed_kernel,
            scal,
            steps,
            [
                (n_b[stream], spec(D)),
                (inv_b[stream], spec(1)),
                (low_b[stream], spec(D)),
                (cots[stream], spec(D)),
                (row_ok[stream], spec(1)),
                (ffn_up, full_spec(ffn_up.shape, stream)),
                (ffn_down, full_spec(ffn_down.shape, stream)),
            ]
            + whole(ffn_parts[stream])
            + whole([bias, vec]),
            [
                ((count, D), F32, spec(D)),
                ((count, FF), BF16, spec(FF)),
                ((count, FF), BF16, spec(FF)),
                ((count, D), BF16, spec(D)),
                ((count, D), F32, spec(D)),
                ((count, D), BF16, spec(D)),
                ((8, D), F32, full_spec((8, D))),
                ((1, FF), F32, full_spec((1, FF))),
            ],
            [
                pltpu.VMEM((D, UNITS), BF16),
                pltpu.VMEM((UNITS, D), BF16),
                pltpu.VMEM((tall, FF), F32),
            ],
            2 * count * D * FF * 8,
            "feed",
        )
        act, dhid, dbr = fed[stream][1:4]
        send, keep = grads_unit(
            scal,
            links.ndp,
            [([(0, 1)], UNITS), ([(2, 3)], UNITS)],
            [low_b[stream], dhid, dbr, act],
        )
        rest = list(range(2, links.bits))
        order = ["m", 1] + rest if stream else [1, "m"] + rest
        reduced_ffn[stream] = links.reduce(send, keep, order)

    total_b = [fed[s][4] for s in range(2)]
    low_total_b = [fed[s][5] for s in range(2)]
    flops = 2 * row_total * D * 8 * HALF * 4
    grad_vec = vectors(none, none, gain[0])
    back = call(
        partial(block_backward_kernel, False),
        scal,
        steps,
        [key_operand]
        + streams(total_b)
        + streams(low_total_b)
        + streams(qkv_b)
        + own_weights(1)
        + own_weights(2)
        + whole(self_parts)
        + streams(n_a)
        + streams(inv_a)
        + whole([grad_vec, grad_vec]),
        stream_outs(6 * HALF, BF16)
        + [((1, 6 * HALF), F32, full_spec((1, 6 * HALF)))] * 2
        + stream_outs(D, F32)
        + stream_outs(D, BF16)
        + [((8, D), F32, full_spec((8, D)))],
        [pltpu.VMEM((rows[0], D), BF16), pltpu.VMEM((rows[1], D), BF16)] + weight_scratch(2),
        flops,
        "self_backward",
    )
    dqkv_b, in_sums_b, total_a, low_total_a, sums_a = (
        back[0:2],
        back[2:4],
        back[4:6],
        back[6:8],
        back[8],
    )
    send, keep = grads_unit(
        scal,
        links.ndp,
        [
            ([(0, 1)], 3 * HALF),
            ([(2, 3)], HALF),
            ([(4, 5)], 3 * HALF),
            ([(6, 7)], HALF),
        ],
        [
            low_a[0],
            dqkv_b[0],
            low_total_b[0],
            o_b[0],
            low_a[1],
            dqkv_b[1],
            low_total_b[1],
            o_b[1],
        ],
    )
    reduced_self = links.reduce(
        send, keep, [2, "m", 1] + list(range(3, links.bits)) if links.bits > 2 else ["m", 1]
    )

    back = call(
        partial(block_backward_kernel, True),
        scal,
        steps,
        [key_operand]
        + streams(total_a)
        + streams(low_total_a)
        + streams(qkv_a)
        + own_weights(0)
        + whole(cross_parts),
        stream_outs(6 * HALF, BF16)
        + [((1, 6 * HALF), F32, full_spec((1, 6 * HALF)))] * 2
        + stream_outs(D, F32),
        [pltpu.VMEM((rows[0], D), BF16), pltpu.VMEM((rows[1], D), BF16)] + weight_scratch(1),
        flops,
        "cross_backward",
    )
    dqkv_a, in_sums_a, grad_rows = back[0:2], back[2:4], back[4:6]
    send, keep = grads_unit(
        scal,
        links.ndp,
        [([(0, 1), (4, 5)], 3 * HALF), ([(2, 3), (6, 7)], HALF)],
        [
            lang,
            dqkv_a[0],
            low_total_a[0],
            o_a[0],
            vision,
            dqkv_a[1],
            low_total_a[1],
            o_a[1],
        ],
    )
    reduced_cross = links.reduce(send, keep, ["m"] + list(range(1, links.bits)))

    ins = [reduced_cross, reduced_self[:, : 4 * HALF], reduced_self[:, 4 * HALF :]]
    low_rows = D // links.ndp
    att_in_grad = jnp.stack(
        [v[:, : 3 * HALF].reshape(low_rows, 3, HALF).transpose(1, 0, 2) for v in ins]
    )
    att_out_grad = jnp.stack([v[:, 3 * HALF :].T for v in ins])
    up_grad = jnp.stack([v[:, :UNITS] for v in reduced_ffn])
    down_grad = jnp.stack([v[:, UNITS:].T for v in reduced_ffn])

    def in_order(value, width):
        lead = value.shape[:-1]
        split = value.reshape(*lead, 2, width)
        swapped = split[..., ::-1, :]
        return jnp.where(links.mp == 0, split, swapped).reshape(value.shape)

    in_sums = jnp.stack([in_sums_a[0] + in_sums_a[1], in_sums_b[0], in_sums_b[1]])
    in_sums = in_sums.reshape(3, 2, 3, HALF)[:, :, ::2].transpose(0, 2, 1, 3).reshape(3, 2, D)
    up_sums = jnp.concatenate([fed[s][7] for s in range(2)])
    parts = (
        in_order(in_sums, HALF),
        in_order(up_sums, UNITS),
        jnp.stack((sums_a[0:2], fed[0][6][3:5], fed[1][6][3:5])),
        jnp.stack((sums_a[2], fed[0][6][5], fed[1][6][5])),
        jnp.stack([fed[s][6][0:2] for s in range(2)]),
        jnp.stack([fed[s][6][2] for s in range(2)]),
    )
    flat = links.total(jnp.concatenate([part.reshape(-1) for part in parts]))
    summed, at = [], 0
    for part in parts:
        summed.append(flat[at : at + part.size].reshape(part.shape))
        at += part.size
    return (
        fed[0][0],
        fed[1][0],
        grad_rows[0],
        grad_rows[1],
        att_in_grad,
        summed[0],
        att_out_grad,
        summed[2],
        summed[3],
        up_grad,
        summed[1],
        down_grad,
        summed[4],
        summed[5],
    )


def solution(mesh):
    rows = P(("dp", "mp"), None)
    return jax.shard_map(
        per_device,
        mesh=mesh,
        in_specs=(
            rows,
            rows,
            P("dp"),
            P(None, None, None, "mp"),
            P(None, None, "mp"),
            P(None, "mp", None),
            P(),
            P(),
            P(None, None, "mp"),
            P(None, "mp"),
            P(None, "mp", None),
            P(),
            P(),
            rows,
            rows,
        ),
        out_specs=(
            rows,
            rows,
            rows,
            rows,
            P(None, None, "dp", "mp"),
            P(),
            P(None, "mp", "dp"),
            P(),
            P(),
            P(None, "dp", "mp"),
            P(),
            P(None, "mp", "dp"),
            P(),
            P(),
        ),
        check_vma=False,
    )
```
